128 devices in a mesh: ublk: 16 (over x, z), salt: 8 (over y, core).
Axes of the slice: x: 4, y: 4, z: 4, core: 2. Of those that a mesh axis runs over, the one named last changes fastest.
Arguments:
- user_factors: bfloat16 [16, 8192, 256], P('ublk', 'salt')
- tile_users: int32 [16, 8, 4096], P('ublk', 'salt'), may hold values from 0 to 8191
- tile_items: int32 [16, 8, 4096], P('ublk', 'salt'), may hold values from 0 to 511
- tile_weight: float32 [16, 8, 4096], P('ublk', 'salt'), may hold values from 0.5 to 8
- live_count: int32 [16, 8], P('ublk', 'salt'), may hold values from 2048 to 4096, as said below
Outputs:
- item_factors: float32 [8, 512, 256], P('salt', 'ublk')
- residual: float32 [8, 512, 256], P('salt', 'ublk')
The draws below stay inside these ranges and needn't reach their ends.
Inputs may be any that keep to these rules, and one draw needn't show every extreme that they name: Every entry of live_count is at least 2048 and at most 4096; some tile is full.
All inputs are finite; a program needn't handle non-finite values.
Results may differ from the reference program's by a relative error of at most 0.0022.
Values may be sent and summed in bfloat16 or wider, within the bound.
A program may use at most 64 MiB of HBM per device.

```python
import math
import jax
import jax.numpy as jnp
import numpy as np
from jax import lax

K = 256
ITERS = 8
NNZ_DEV = 4096
USER_BLK = 8192
ITEM_SALT = 512
N_UBLK = 16
N_SALT = 8


def draw_user_factors(key, part):
    key_cols, key_rows, key_base = jax.random.split(key, 3)
    cols = jnp.exp(jax.random.uniform(key_cols, (K,), jnp.float32, math.log(0.3), 0.0))
    scales = jnp.exp(jax.random.uniform(key_rows, (N_UBLK, USER_BLK, 1), jnp.float32, math.log(0.3), math.log(3.0)))
    base = jax.random.normal(key_base, (N_UBLK, USER_BLK, K), jnp.float32)
    values = base * cols * scales / jnp.sqrt(jnp.float32(N_UBLK * USER_BLK))
    return values.astype(jnp.bfloat16)


def draw_live_count(key, part):
    key_counts, key_full = jax.random.split(jax.random.fold_in(key, 17))
    counts = jax.random.randint(key_counts, (N_UBLK * N_SALT,), NNZ_DEV // 2, NNZ_DEV + 1)
    chosen = jax.random.randint(key_full, (), 0, N_UBLK * N_SALT)
    positions = jnp.arange(N_UBLK * N_SALT)
    counts = jnp.where(positions == chosen, NNZ_DEV, counts)
    return counts.reshape(N_UBLK, N_SALT).astype(jnp.int32)


def place_ends(result, own_key, smallest, top_value):
    extent = result.shape
    index_at = [jax.random.randint(jax.random.fold_in(own_key, axis), (), 0, extent[axis]) for axis in range(len(extent))]
    result = result.at[tuple(index_at)].set(smallest)
    longest = extent.index(max(extent))
    index_at[longest] = (index_at[longest] + 1) % extent[longest]
    return result.at[tuple(index_at)].set(top_value)


def levels(stream_key, shape, cuts, smallest, high):
    gain = 1.0
    for axis_at, shards_of in cuts:
        heights = jax.random.uniform(jax.random.fold_in(jax.random.fold_in(stream_key, 6), axis_at), (shards_of,), jnp.float32, smallest / len(cuts), high / len(cuts))
        gain = gain * jnp.repeat(jnp.exp(heights), shape[axis_at] // shards_of).reshape((-1,) + (1,) * (len(shape) - 1 - axis_at))
    return gain


def rank_bounds(amount, skew):
    portions = [(1 << 20) // math.isqrt(grade ** skew) + 1 for grade in range(1, amount + 1)]
    deviation = 1 + sum(portions) // (1 << 30)
    return np.cumsum(np.array([max(1, weight // deviation) for weight in portions]))


def ranked(stream_key, shape, number_of, lean):
    grid = rank_bounds(number_of, lean)
    ticket = jax.random.randint(jax.random.fold_in(stream_key, 1), shape, 0, int(grid[number_of - 1]))
    rank = jnp.searchsorted(jnp.asarray(grid, jnp.int32), ticket, side="right")
    return jax.random.permutation(jax.random.fold_in(stream_key, 2), number_of)[rank].astype(jnp.int32)


def setup_inputs(seed: int = 0) -> dict:
    keys = jax.random.split(jax.random.key(seed), 6)
    user_factors = draw_user_factors(jax.random.fold_in(keys[5], 71), 0)
    tile_users = place_ends(jax.random.randint(keys[1], (N_UBLK, N_SALT, NNZ_DEV), 0, USER_BLK), jax.random.fold_in(keys[1], 1), 0, USER_BLK - 1).astype(jnp.int32)
    tile_items = place_ends(ranked(keys[2], (N_UBLK, N_SALT, NNZ_DEV), ITEM_SALT, 2), jax.random.fold_in(keys[2], 3), 0, ITEM_SALT - 1).astype(jnp.int32)
    tile_weight = jnp.clip(jnp.exp(math.log(8.0) - 2.7725887 * jax.random.uniform(keys[3], (N_UBLK, N_SALT, NNZ_DEV), jnp.float32) ** levels(keys[3], (N_UBLK, N_SALT, NNZ_DEV), ((0, 16), (1, 8)), -0.2, 0.2)), 0.5, 8.0)
    live_count = draw_live_count(jax.random.fold_in(keys[5], 71), 0)
    return {"user_factors": user_factors, "tile_users": tile_users, "tile_items": tile_items, "tile_weight": tile_weight, "live_count": live_count}


REG = 1.0
EPS = 1e-6


def operate(direction, rows, items, weight, gram):
    along = jnp.sum(rows * direction[items], axis=1) * weight
    local = jax.ops.segment_sum(along[:, None] * rows, items, num_segments=direction.shape[0])
    return local + jnp.dot(direction, gram, precision=lax.Precision.HIGHEST) + REG * direction


def reference(user_factors, tile_users, tile_items, tile_weight, live_count):
    flat = user_factors.reshape(N_UBLK * USER_BLK, K)
    gram = jnp.dot(flat.T, flat, preferred_element_type=jnp.float32)
    offsets = (jnp.arange(N_UBLK) * USER_BLK).astype(jnp.int32)
    slots = jnp.arange(NNZ_DEV).astype(jnp.int32)
    solved = []
    leftover = []
    for column in range(N_SALT):
        users = (tile_users[:, column, :] + offsets[:, None]).reshape(-1)
        items = tile_items[:, column, :].reshape(-1)
        live = slots[None, :] < live_count[:, column][:, None]
        raw = tile_weight[:, column, :]
        weight = jnp.where(live, raw, jnp.zeros_like(raw)).reshape(-1)
        confid = jnp.where(live, 1.0 + raw, jnp.zeros_like(raw)).reshape(-1)
        rows = flat[users].astype(jnp.float32)
        rhs = jax.ops.segment_sum(confid[:, None] * rows, items, num_segments=ITEM_SALT)
        solution = jnp.zeros_like(rhs)
        resid = rhs
        direction = rhs
        norm_now = jnp.sum(resid * resid, axis=1)
        for step in range(ITERS):
            image = operate(direction, rows, items, weight, gram)
            alpha = norm_now / (jnp.sum(direction * image, axis=1) + EPS)
            solution = solution + alpha[:, None] * direction
            resid = resid - alpha[:, None] * image
            norm_next = jnp.sum(resid * resid, axis=1)
            direction = resid + (norm_next / (norm_now + EPS))[:, None] * direction
            norm_now = norm_next
        solved.append(solution)
        leftover.append(resid)
    return jnp.stack(solved), jnp.stack(leftover)
```

```python
import jax
import jax.numpy as jnp
from jax import lax
from jax.experimental import pallas as pl
from jax.experimental.pallas import tpu as pltpu
from jax.sharding import PartitionSpec as P

ITERS = 8
REG = 1.0
EPS = 1e-06

X = 4
OWNERS = X * X
OWN = 32
RANK = 256
ITEMS = OWNERS * OWN
SLOTS = 4096
SHARD = 1024
SALT = 8
CHUNKS = 4
CHUNK = SHARD // CHUNKS
TILE = 1024
GRAM_OWN = RANK // OWNERS

F32 = jnp.float32
BF16 = jnp.bfloat16
MESH = pl.DeviceIdType.MESH


def ring(a):
    return min(a, X - a)


OFFSETS = sorted(
    [(dx, dz) for dx in range(X) for dz in range(X)],
    key=lambda o: (ring(o[0]) + ring(o[1]), o),
)
FAR_FIRST = list(range(OWNERS - 1, 0, -1))
GROUPS = [list(range(OWNERS))]

PARTNER, UP, DOWN, ACROSS, P_UP, P_DOWN, P_ACROSS = range(7)


def kernel(
    shard, users, items, raw, live,
    x_out, r_out,
    block, rows_t, scaled_t, rows, mask, terms, gram, gram_sum, gram_in, gram_own,
    rhs, rhs_in, whole_dir, direction, own_terms, out_terms, in_terms,
    ag_send, ag_recv, gram_send, gram_recv, gall_send, gall_recv,
    rhs_send, rhs_recv, dir_send, dir_recv, loc_send, loc_recv,
):
    ublk = lax.axis_index("ublk")
    salt = lax.axis_index("salt")
    px, pz = lax.div(ublk, X), lax.rem(ublk, X)
    py, pc = lax.div(salt, 2), lax.rem(salt, 2)

    def owner(k, sign=1):
        dx, dz = OFFSETS[k]
        return lax.rem(px + sign * dx + X, X) * X + lax.rem(pz + sign * dz + X, X)

    def line(dy, core):
        return lax.rem(py + dy, X) * 2 + core

    def remote(src, dst, send, recv, device):
        copy = pltpu.make_async_remote_copy(
            src_ref=src, dst_ref=dst, send_sem=send, recv_sem=recv,
            device_id=device, device_id_type=MESH,
        )
        return copy

    barrier = pltpu.get_barrier_semaphore()
    peers = [(owner(k), salt) for k in range(1, OWNERS)]
    peers += [(ublk, line(1, pc)), (ublk, line(3, pc)), (ublk, line(0, 1 - pc))]
    for device in peers:
        pl.semaphore_signal(barrier, inc=1, device_id=device, device_id_type=MESH)
    pl.semaphore_wait(barrier, len(peers))

    def piece(ref, h):
        return ref.at[pl.ds(h * CHUNK, CHUNK)]

    def gathered(src, place, h, device):
        return remote(src, piece(block.at[place], h), ag_send.at[place, h], ag_recv.at[place, h], device)

    copies = {}
    for h in range(CHUNKS):
        copies[UP, h] = gathered(piece(shard, h), UP, h, (ublk, line(1, pc)))
        copies[DOWN, h] = gathered(piece(shard, h), DOWN, h, (ublk, line(3, pc)))
        copies[PARTNER, h] = gathered(piece(shard, h), PARTNER, h, (ublk, line(0, 1 - pc)))
        for place in (UP, DOWN, PARTNER):
            copies[place, h].start()

    def relay(h):
        for place in (UP, DOWN):
            copies[place, h].wait_recv()
        copies[ACROSS, h] = gathered(piece(block.at[UP + pc], h), ACROSS, h, (ublk, line(1 + 2 * pc, pc)))
        copies[P_UP, h] = gathered(piece(block.at[UP], h), P_UP, h, (ublk, line(0, 1 - pc)))
        copies[P_DOWN, h] = gathered(piece(block.at[DOWN], h), P_DOWN, h, (ublk, line(0, 1 - pc)))
        for place in (ACROSS, P_UP, P_DOWN):
            copies[place, h].start()

    def relay_across(h):
        copies[ACROSS, h].wait_recv()
        copies[P_ACROSS, h] = gathered(piece(block.at[ACROSS], h), P_ACROSS, h, (ublk, line(0, 1 - pc)))
        copies[P_ACROSS, h].start()

    def arrived(place):
        for h in range(CHUNKS):
            copies[place, h].wait_recv()

    def select(source, who, first=False):
        part = source[...]
        part_t = part.T
        outer = jnp.dot(part_t, part, preferred_element_type=F32)
        if first:
            gram[...] = outer
        else:
            gram[...] += outer
        base = who * SHARD

        def step(n, carry):
            at = pl.ds(pl.multiple_of(n * TILE, TILE), TILE)
            place = users[:, at] - base
            chosen = place == lax.broadcasted_iota(jnp.int32, (SHARD, TILE), 0)
            one_hot = jnp.where(chosen, 1.0, 0.0).astype(BF16)
            found = jnp.dot(part_t, one_hot, preferred_element_type=F32).astype(BF16)
            if first:
                rows_t[:, at] = found
            else:
                rows_t[:, at] += found
            return carry

        lax.fori_loop(0, SLOTS // TILE, step, 0)

    select(shard, salt, first=True)
    arrived(PARTNER)
    select(block.at[PARTNER], line(0, 1 - pc))
    for h in range(CHUNKS // 2):
        relay(h)
    for k in range(OWNERS):
        place = items[...] - owner(k) * OWN
        chosen = place == lax.broadcasted_iota(jnp.int32, (OWN, SLOTS), 0)
        mask[pl.ds(k * OWN, OWN)] = jnp.where(chosen, 1.0, 0.0).astype(BF16)
    for h in range(CHUNKS // 2, CHUNKS):
        relay(h)
    select(block.at[UP], line(3, pc))
    select(block.at[DOWN], line(1, pc))
    for h in range(CHUNKS // 2):
        relay_across(h)
    arrived(P_UP)
    select(block.at[P_UP], line(3, 1 - pc))
    for h in range(CHUNKS // 2, CHUNKS):
        relay_across(h)
    arrived(P_DOWN)
    select(block.at[P_DOWN], line(1, 1 - pc))
    select(block.at[ACROSS], line(2, pc))
    arrived(P_ACROSS)
    select(block.at[P_ACROSS], line(2, 1 - pc))

    gram_copies = [
        remote(
            gram.at[pl.ds(pl.multiple_of(owner(k) * GRAM_OWN, GRAM_OWN), GRAM_OWN)], gram_in.at[k],
            gram_send.at[k], gram_recv.at[k], (owner(k), salt),
        )
        for k in range(OWNERS) if k
    ]
    for copy in reversed(gram_copies):
        copy.start()

    alive = lax.broadcasted_iota(jnp.int32, (1, SLOTS), 1) < live[0, 0]
    weight = jnp.where(alive, raw[...], 0.0)
    confid = jnp.where(alive, 1.0 + raw[...], 0.0)
    for n in range(SLOTS // TILE):
        at = pl.ds(n * TILE, TILE)
        rows[at] = rows_t[:, at].T
        scaled_t[:, at] = (rows_t[:, at].astype(F32) * weight[:, n * TILE:(n + 1) * TILE]).astype(BF16)

    upper = confid.astype(BF16)
    lower = (confid - upper.astype(F32)).astype(BF16)
    for step, level in enumerate((upper, lower)):
        for n in range(SLOTS // TILE):
            at = pl.ds(n * TILE, TILE)
            terms[:, at] = jnp.where(mask[:, at] != 0, level[:, n * TILE:(n + 1) * TILE], jnp.zeros((), BF16))
        part = jnp.dot(terms[...], rows[...], preferred_element_type=F32)
        if step == 0:
            rhs[...] = part
        else:
            rhs[...] += part

    rhs_copies = [
        remote(
            rhs.at[pl.ds(k * OWN, OWN)], rhs_in.at[k], rhs_send.at[k], rhs_recv.at[k], (owner(k), salt)
        )
        for k in range(OWNERS) if k
    ]
    for copy in reversed(rhs_copies):
        copy.start()

    own_rows = pl.ds(pl.multiple_of(ublk * GRAM_OWN, GRAM_OWN), GRAM_OWN)
    total = gram[own_rows]
    for k in range(1, OWNERS):
        gram_copies[k - 1].wait_recv()
        total = total + gram_in[k]
    gram_own[...] = total
    gram_sum[own_rows] = total
    gall_copies = [
        remote(
            gram_own, gram_sum.at[own_rows], gall_send.at[k], gall_recv.at[k], (owner(k), salt)
        )
        for k in range(OWNERS) if k
    ]
    for copy in reversed(gall_copies):
        copy.start()

    total = rhs[pl.ds(0, OWN)]
    for k in range(1, OWNERS):
        rhs_copies[k - 1].wait_recv()
        total = total + rhs_in[k]
    direction[...] = total
    r_out[...] = total
    x_out[...] = jnp.zeros_like(total)
    whole_dir[pl.ds(0, OWN)] = total.astype(BF16)

    def iteration(t, carry):
        dir_copies = {
            k: remote(
                whole_dir.at[pl.ds(0, OWN)], whole_dir.at[pl.ds(k * OWN, OWN)],
                dir_send.at[k], dir_recv.at[k], (owner(k, -1), salt),
            )
            for k in range(1, OWNERS)
        }
        loc_copies = {
            k: remote(
                out_terms.at[pl.ds(k * OWN, OWN)], in_terms.at[k],
                loc_send.at[k], loc_recv.at[k], (owner(k), salt),
            )
            for k in range(1, OWNERS)
        }
        for k in FAR_FIRST:
            dir_copies[k].start()
        for group in GROUPS:
            for k in group:
                if k:
                    dir_copies[k].wait_recv()
            at = pl.ds(group[0] * OWN, len(group) * OWN)
            for n in range(SLOTS // TILE):
                cols = pl.ds(n * TILE, TILE)
                along = jnp.dot(whole_dir[at], scaled_t[:, cols], preferred_element_type=F32)
                terms[at, cols] = jnp.where(mask[at, cols] != 0, along.astype(BF16), jnp.zeros((), BF16))
            local = jnp.dot(terms[at], rows[...], preferred_element_type=F32)
            if group[0] == 0:
                own_terms[...] = local[:OWN]
            out_terms[at] = local.astype(BF16)
            for k in reversed(group):
                if k:
                    loc_copies[k].start()

        @pl.when(t == 0)
        def _():
            for copy in gall_copies:
                copy.wait_recv()

        p = direction[...]
        r = r_out[...]
        norm_now = jnp.sum(r * r, axis=1, keepdims=True)
        image = jnp.dot(p, gram_sum[...], precision=lax.Precision.HIGHEST, preferred_element_type=F32) + REG * p
        image = image + own_terms[...]
        for k in range(1, OWNERS):
            dir_copies[k].wait_send()
        for k in range(1, OWNERS):
            loc_copies[k].wait_recv()
            image = image + in_terms[k].astype(F32)
        alpha = norm_now / (jnp.sum(p * image, axis=1, keepdims=True) + EPS)
        x_out[...] += alpha * p
        r = r - alpha * image
        r_out[...] = r
        norm_next = jnp.sum(r * r, axis=1, keepdims=True)
        p = r + (norm_next / (norm_now + EPS)) * p
        direction[...] = p
        whole_dir[pl.ds(0, OWN)] = p.astype(BF16)
        for k in range(1, OWNERS):
            loc_copies[k].wait_send()
        return carry

    lax.fori_loop(0, ITERS, iteration, 0)

    for copy in list(copies.values()) + gram_copies + gall_copies + rhs_copies:
        copy.wait_send()


def body(user_factors, tile_users, tile_items, tile_weight, live_count):
    vmem = pl.BlockSpec(memory_space=pltpu.VMEM)
    dma = pltpu.SemaphoreType.DMA
    found, left = pl.pallas_call(
        kernel,
        name="als_cg",
        out_shape=(jax.ShapeDtypeStruct((OWN, RANK), F32), jax.ShapeDtypeStruct((OWN, RANK), F32)),
        in_specs=[vmem, vmem, vmem, vmem, pl.BlockSpec(memory_space=pltpu.SMEM)],
        out_specs=(vmem, vmem),
        scratch_shapes=[
            pltpu.VMEM((SALT - 1, SHARD, RANK), BF16),
            pltpu.VMEM((RANK, SLOTS), BF16),
            pltpu.VMEM((RANK, SLOTS), BF16),
            pltpu.VMEM((SLOTS, RANK), BF16),
            pltpu.VMEM((ITEMS, SLOTS), BF16),
            pltpu.VMEM((ITEMS, SLOTS), BF16),
            pltpu.VMEM((RANK, RANK), F32),
            pltpu.VMEM((RANK, RANK), F32),
            pltpu.VMEM((OWNERS, GRAM_OWN, RANK), F32),
            pltpu.VMEM((GRAM_OWN, RANK), F32),
            pltpu.VMEM((ITEMS, RANK), F32),
            pltpu.VMEM((OWNERS, OWN, RANK), F32),
            pltpu.VMEM((ITEMS, RANK), BF16),
            pltpu.VMEM((OWN, RANK), F32),
            pltpu.VMEM((OWN, RANK), F32),
            pltpu.VMEM((ITEMS, RANK), BF16),
            pltpu.VMEM((OWNERS, OWN, RANK), BF16),
            dma((SALT - 1, CHUNKS)), dma((SALT - 1, CHUNKS)),
            dma((OWNERS,)), dma((OWNERS,)), dma((OWNERS,)), dma((OWNERS,)),
            dma((OWNERS,)), dma((OWNERS,)), dma((OWNERS,)), dma((OWNERS,)),
            dma((OWNERS,)), dma((OWNERS,)),
        ],
        compiler_params=pltpu.CompilerParams(
            collective_id=0, has_side_effects=True, vmem_limit_bytes=56 * 2**20
        ),
    )(user_factors[0], tile_users[0], tile_items[0], tile_weight[0], live_count)
    return (found[None], left[None])


def solution(mesh):
    return jax.shard_map(
        body,
        mesh=mesh,
        in_specs=(
            P("ublk", "salt", None),
            P("ublk", "salt", None),
            P("ublk", "salt", None),
            P("ublk", "salt", None),
            P("ublk", "salt"),
        ),
        out_specs=(P("salt", "ublk", None), P("salt", "ublk", None)),
        check_vma=False,
    )
```

```python
import jax
import jax.numpy as jnp
from jax import lax
from jax.experimental import pallas as pl
from jax.experimental.pallas import tpu as pltpu
from jax.sharding import PartitionSpec as P

ITERS = 8
REG = 1.0
EPS = 1e-06

X = 4
OWNERS = X * X
OWN = 32
RANK = 256
ITEMS = OWNERS * OWN
SLOTS = 4096
SHARD = 1024
SALT = 8
CHUNKS = 4
CHUNK = SHARD // CHUNKS
TILE = 1024
GRAM_OWN = RANK // OWNERS

F32 = jnp.float32
BF16 = jnp.bfloat16
MESH = pl.DeviceIdType.MESH


def ring(a):
    return min(a, X - a)


OFFSETS = sorted(
    [(dx, dz) for dx in range(X) for dz in range(X)],
    key=lambda o: (ring(o[0]) + ring(o[1]), o),
)
FAR_FIRST = list(range(OWNERS - 1, 0, -1))
GROUPS = 2
HALF = OWN // GROUPS
GROUP = OWNERS * HALF
UNIT = 512

PARTNER, UP, DOWN, ACROSS, P_UP, P_DOWN, P_ACROSS = range(7)


def kernel(
    shard, users, items, raw, live,
    x_out, r_out,
    block, weight, confid, rows_t, scaled_t, rows, mask, terms, gram, gram_sum, gram_in, gram_own,
    rhs, rhs_in, whole_dir, direction, own_terms, out_terms, in_terms,
    ag_send, ag_recv, gram_send, gram_recv, gall_send, gall_recv,
    rhs_send, rhs_recv, dir_send, dir_recv, loc_send, loc_recv,
):
    ublk = lax.axis_index("ublk")
    salt = lax.axis_index("salt")
    px, pz = lax.div(ublk, X), lax.rem(ublk, X)
    py, pc = lax.div(salt, 2), lax.rem(salt, 2)

    def owner(k, sign=1):
        dx, dz = OFFSETS[k]
        return lax.rem(px + sign * dx + X, X) * X + lax.rem(pz + sign * dz + X, X)

    def line(dy, core):
        return lax.rem(py + dy, X) * 2 + core

    def remote(src, dst, send, recv, device):
        copy = pltpu.make_async_remote_copy(
            src_ref=src, dst_ref=dst, send_sem=send, recv_sem=recv,
            device_id=device, device_id_type=MESH,
        )
        return copy

    barrier = pltpu.get_barrier_semaphore()
    peers = [(owner(k), salt) for k in range(1, OWNERS)]
    peers += [(ublk, line(1, pc)), (ublk, line(3, pc)), (ublk, line(0, 1 - pc))]
    for device in peers:
        pl.semaphore_signal(barrier, inc=1, device_id=device, device_id_type=MESH)

    for g in range(GROUPS):
        for k in range(OWNERS):
            place = items[...] - (owner(k) * OWN + g * HALF)
            chosen = place == lax.broadcasted_iota(jnp.int32, (HALF, SLOTS), 0)
            mask[pl.ds(g * GROUP + k * HALF, HALF)] = jnp.where(chosen, 1.0, 0.0).astype(BF16)
    alive = lax.broadcasted_iota(jnp.int32, (1, SLOTS), 1) < live[0, 0]
    weight[...] = jnp.where(alive, raw[...], 0.0)
    confid[...] = jnp.where(alive, 1.0 + raw[...], 0.0)

    def select(source, who, unit, first=False, last=None):
        part = source[pl.ds(unit * UNIT, UNIT)]
        part_t = part.T
        outer = jnp.dot(part_t, part, preferred_element_type=F32)
        if first:
            gram[...] = outer
        else:
            gram[...] += outer
        if last is not None:
            last()
        base = who * SHARD + unit * UNIT
        for n in range(SLOTS // TILE):
            at = pl.ds(n * TILE, TILE)
            chosen = (users[:, at] - base) == lax.broadcasted_iota(jnp.int32, (UNIT, TILE), 0)
            one_hot = jnp.where(chosen, 1.0, 0.0).astype(BF16)
            found = jnp.dot(part_t, one_hot, preferred_element_type=F32).astype(BF16)
            if not first:
                found = rows_t[:, at] + found
            if last is None:
                rows_t[:, at] = found
            else:
                rows[at] = found.T
                scaled_t[:, at] = (found.astype(F32) * weight[:, at]).astype(BF16)

    select(shard, salt, 0, first=True)
    pl.semaphore_wait(barrier, len(peers))

    def piece(ref, h):
        return ref.at[pl.ds(h * CHUNK, CHUNK)]

    def gathered(src, place, h, device):
        return remote(src, piece(block.at[place], h), ag_send.at[place, h], ag_recv.at[place, h], device)

    copies = {}
    for h in range(CHUNKS):
        copies[UP, h] = gathered(piece(shard, h), UP, h, (ublk, line(1, pc)))
        copies[DOWN, h] = gathered(piece(shard, h), DOWN, h, (ublk, line(3, pc)))
        copies[PARTNER, h] = gathered(piece(shard, h), PARTNER, h, (ublk, line(0, 1 - pc)))
        for place in (UP, DOWN, PARTNER):
            copies[place, h].start()

    def relay(h):
        for place in (UP, DOWN):
            copies[place, h].wait_recv()
        copies[ACROSS, h] = gathered(piece(block.at[UP + pc], h), ACROSS, h, (ublk, line(1 + 2 * pc, pc)))
        copies[P_UP, h] = gathered(piece(block.at[UP], h), P_UP, h, (ublk, line(0, 1 - pc)))
        copies[P_DOWN, h] = gathered(piece(block.at[DOWN], h), P_DOWN, h, (ublk, line(0, 1 - pc)))
        for place in (ACROSS, P_UP, P_DOWN):
            copies[place, h].start()

    def relay_across(h):
        copies[ACROSS, h].wait_recv()
        copies[P_ACROSS, h] = gathered(piece(block.at[ACROSS], h), P_ACROSS, h, (ublk, line(0, 1 - pc)))
        copies[P_ACROSS, h].start()

    whose = {
        PARTNER: line(0, 1 - pc), UP: line(3, pc), DOWN: line(1, pc), ACROSS: line(2, pc),
        P_UP: line(3, 1 - pc), P_DOWN: line(1, 1 - pc), P_ACROSS: line(2, 1 - pc),
    }

    def take(place, unit, last=None):
        if place in (PARTNER, P_UP, P_DOWN, P_ACROSS):
            for h in range(unit * UNIT // CHUNK, (unit + 1) * UNIT // CHUNK):
                copies[place, h].wait_recv()
        select(block.at[place], whose[place], unit, last=last)

    gram_copies = [
        remote(
            gram.at[pl.ds(pl.multiple_of(owner(k) * GRAM_OWN, GRAM_OWN), GRAM_OWN)], gram_in.at[k],
            gram_send.at[k], gram_recv.at[k], (owner(k), salt),
        )
        for k in range(OWNERS) if k
    ]

    def send_gram():
        for copy in reversed(gram_copies):
            copy.start()

    select(shard, salt, 1)
    take(PARTNER, 0)
    take(PARTNER, 1)
    relay(0)
    relay(1)
    take(UP, 0)
    relay(2)
    take(DOWN, 0)
    take(P_UP, 0)
    relay(3)
    take(P_DOWN, 0)
    take(UP, 1)
    relay_across(0)
    take(DOWN, 1)
    relay_across(1)
    take(P_UP, 1)
    relay_across(2)
    take(P_DOWN, 1)
    relay_across(3)
    take(ACROSS, 0)
    take(P_ACROSS, 0)
    take(ACROSS, 1)
    take(P_ACROSS, 1, last=send_gram)

    upper = confid[...].astype(BF16)
    lower = (confid[...] - upper.astype(F32)).astype(BF16)
    rhs_copies = {}
    for g in range(GROUPS):
        at = pl.ds(g * GROUP, GROUP)
        parts = []
        for level in (upper, lower):
            for n in range(SLOTS // TILE):
                cols = pl.ds(n * TILE, TILE)
                terms[at, cols] = jnp.where(
                    mask[at, cols] != 0, level[:, n * TILE:(n + 1) * TILE], jnp.zeros((), BF16)
                )
            parts.append(jnp.dot(terms[at], rows[...], preferred_element_type=F32))
        rhs[at] = parts[0] + parts[1]
        for k in FAR_FIRST:
            rhs_copies[g, k] = remote(
                rhs.at[pl.ds(g * GROUP + k * HALF, HALF)], rhs_in.at[g, k],
                rhs_send.at[g, k], rhs_recv.at[g, k], (owner(k), salt),
            )
            rhs_copies[g, k].start()

    own_rows = pl.ds(pl.multiple_of(ublk * GRAM_OWN, GRAM_OWN), GRAM_OWN)
    total = gram[own_rows]
    for k in range(1, OWNERS):
        gram_copies[k - 1].wait_recv()
        total = total + gram_in[k]
    gram_own[...] = total
    gram_sum[own_rows] = total
    gall_copies = [
        remote(
            gram_own, gram_sum.at[own_rows], gall_send.at[k], gall_recv.at[k], (owner(k), salt)
        )
        for k in range(OWNERS) if k
    ]

    dir_copies = {}
    loc_copies = {}
    for g in range(GROUPS):
        for k in range(1, OWNERS):
            dir_copies[g, k] = remote(
                whole_dir.at[pl.ds(g * GROUP, HALF)], whole_dir.at[pl.ds(g * GROUP + k * HALF, HALF)],
                dir_send.at[g, k], dir_recv.at[g, k], (owner(k, -1), salt),
            )
            loc_copies[g, k] = remote(
                out_terms.at[pl.ds(g * GROUP + k * HALF, HALF)], in_terms.at[g, k],
                loc_send.at[g, k], loc_recv.at[g, k], (owner(k), salt),
            )

    def send_direction(g, p):
        direction[pl.ds(g * HALF, HALF)] = p
        whole_dir[pl.ds(g * GROUP, HALF)] = p.astype(BF16)
        for k in FAR_FIRST:
            dir_copies[g, k].start()

    for g in range(GROUPS):
        own = pl.ds(g * HALF, HALF)
        total = rhs[pl.ds(g * GROUP, HALF)]
        for k in range(1, OWNERS):
            rhs_copies[g, k].wait_recv()
            total = total + rhs_in[g, k]
        send_direction(g, total)
        r_out[own] = total
        x_out[own] = jnp.zeros_like(total)
        if g == 0:
            for copy in reversed(gall_copies):
                copy.start()

    def iteration(t, carry):
        for g in range(GROUPS):
            at = pl.ds(g * GROUP, GROUP)
            for k in range(1, OWNERS):
                dir_copies[g, k].wait_recv()
            for n in range(SLOTS // TILE):
                cols = pl.ds(n * TILE, TILE)
                along = jnp.dot(whole_dir[at], scaled_t[:, cols], preferred_element_type=F32)
                terms[at, cols] = jnp.where(mask[at, cols] != 0, along.astype(BF16), jnp.zeros((), BF16))
            local = jnp.dot(terms[at], rows[...], preferred_element_type=F32)
            own_terms[pl.ds(g * HALF, HALF)] = local[:HALF]
            out_terms[at] = local.astype(BF16)
            for k in FAR_FIRST:
                loc_copies[g, k].start()

        @pl.when(t == 0)
        def _():
            for copy in gall_copies:
                copy.wait_recv()

        for g in range(GROUPS):
            own = pl.ds(g * HALF, HALF)
            p = direction[own]
            r = r_out[own]
            norm_now = jnp.sum(r * r, axis=1, keepdims=True)
            image = jnp.dot(p, gram_sum[...], precision=lax.Precision.HIGHEST, preferred_element_type=F32)
            image = image + REG * p + own_terms[own]
            for k in range(1, OWNERS):
                dir_copies[g, k].wait_send()
            for k in range(1, OWNERS):
                loc_copies[g, k].wait_recv()
                image = image + in_terms[g, k].astype(F32)
            alpha = norm_now / (jnp.sum(p * image, axis=1, keepdims=True) + EPS)
            x_out[own] += alpha * p
            r = r - alpha * image
            r_out[own] = r
            norm_next = jnp.sum(r * r, axis=1, keepdims=True)

            @pl.when(t < ITERS - 1)
            def _():
                send_direction(g, r + (norm_next / (norm_now + EPS)) * p)

            for k in range(1, OWNERS):
                loc_copies[g, k].wait_send()
        return carry

    lax.fori_loop(0, ITERS, iteration, 0)

    for copy in list(copies.values()) + gram_copies + gall_copies + list(rhs_copies.values()):
        copy.wait_send()


def body(user_factors, tile_users, tile_items, tile_weight, live_count):
    vmem = pl.BlockSpec(memory_space=pltpu.VMEM)
    dma = pltpu.SemaphoreType.DMA
    found, left = pl.pallas_call(
        kernel,
        name="als_cg",
        out_shape=(jax.ShapeDtypeStruct((OWN, RANK), F32), jax.ShapeDtypeStruct((OWN, RANK), F32)),
        in_specs=[vmem, vmem, vmem, vmem, pl.BlockSpec(memory_space=pltpu.SMEM)],
        out_specs=(vmem, vmem),
        scratch_shapes=[
            pltpu.VMEM((SALT - 1, SHARD, RANK), BF16),
            pltpu.VMEM((1, SLOTS), F32),
            pltpu.VMEM((1, SLOTS), F32),
            pltpu.VMEM((RANK, SLOTS), BF16),
            pltpu.VMEM((RANK, SLOTS), BF16),
            pltpu.VMEM((SLOTS, RANK), BF16),
            pltpu.VMEM((ITEMS, SLOTS), BF16),
            pltpu.VMEM((ITEMS, SLOTS), BF16),
            pltpu.VMEM((RANK, RANK), F32),
            pltpu.VMEM((RANK, RANK), F32),
            pltpu.VMEM((OWNERS, GRAM_OWN, RANK), F32),
            pltpu.VMEM((GRAM_OWN, RANK), F32),
            pltpu.VMEM((ITEMS, RANK), F32),
            pltpu.VMEM((GROUPS, OWNERS, HALF, RANK), F32),
            pltpu.VMEM((ITEMS, RANK), BF16),
            pltpu.VMEM((OWN, RANK), F32),
            pltpu.VMEM((OWN, RANK), F32),
            pltpu.VMEM((ITEMS, RANK), BF16),
            pltpu.VMEM((GROUPS, OWNERS, HALF, RANK), BF16),
            dma((SALT - 1, CHUNKS)), dma((SALT - 1, CHUNKS)),
            dma((OWNERS,)), dma((OWNERS,)), dma((OWNERS,)), dma((OWNERS,)),
            dma((GROUPS, OWNERS)), dma((GROUPS, OWNERS)), dma((GROUPS, OWNERS)), dma((GROUPS, OWNERS)),
            dma((GROUPS, OWNERS)), dma((GROUPS, OWNERS)),
        ],
        compiler_params=pltpu.CompilerParams(
            collective_id=0, has_side_effects=True, vmem_limit_bytes=56 * 2**20
        ),
    )(user_factors[0], tile_users[0], tile_items[0], tile_weight[0], live_count)
    return (found[None], left[None])


def solution(mesh):
    return jax.shard_map(
        body,
        mesh=mesh,
        in_specs=(
            P("ublk", "salt", None),
            P("ublk", "salt", None),
            P("ublk", "salt", None),
            P("ublk", "salt", None),
            P("ublk", "salt"),
        ),
        out_specs=(P("salt", "ublk", None), P("salt", "ublk", None)),
        check_vma=False,
    )
```

```python
import jax
import jax.numpy as jnp
from jax import lax
from jax.experimental import pallas as pl
from jax.experimental.pallas import tpu as pltpu
from jax.sharding import PartitionSpec as P

ITERS = 8
REG = 1.0
EPS = 1e-06

X = 4
OWNERS = X * X
OWN = 32
RANK = 256
ITEMS = OWNERS * OWN
SLOTS = 4096
SHARD = 1024
SALT = 8
CHUNKS = 4
CHUNK = SHARD // CHUNKS
TILE = 1024
GRAM_OWN = RANK // OWNERS

F32 = jnp.float32
BF16 = jnp.bfloat16
MESH = pl.DeviceIdType.MESH


def ring(a):
    return min(a, X - a)


OFFSETS = sorted(
    [(dx, dz) for dx in range(X) for dz in range(X)],
    key=lambda o: (ring(o[0]) + ring(o[1]), o),
)
FAR_FIRST = list(range(OWNERS - 1, 0, -1))
GROUPS = 2
HALF = OWN // GROUPS
GROUP = OWNERS * HALF
PARTS = (range(0, OWNERS // 2), range(OWNERS // 2, OWNERS))
UNIT = 512

PARTNER, UP, DOWN, ACROSS, P_UP, P_DOWN, P_ACROSS = range(7)


def kernel(
    shard_in, users_in, items_in, raw_in, live,
    x_out, r_out,
    shard, users, items, raw, load_sem, block, weight, confid, rows_t, scaled_t, rows, mask, terms, gram, gram_sum, gram_in, gram_own,
    rhs, rhs_in, whole_dir, direction, own_terms, out_terms, in_terms,
    ag_send, ag_recv, gram_send, gram_recv, gall_send, gall_recv,
    rhs_send, rhs_recv, dir_send, dir_recv, loc_send, loc_recv,
):
    ublk = lax.axis_index("ublk")
    salt = lax.axis_index("salt")
    px, pz = lax.div(ublk, X), lax.rem(ublk, X)
    py, pc = lax.div(salt, 2), lax.rem(salt, 2)

    def owner(k, sign=1):
        dx, dz = OFFSETS[k]
        return lax.rem(px + sign * dx + X, X) * X + lax.rem(pz + sign * dz + X, X)

    def line(dy, core):
        return lax.rem(py + dy, X) * 2 + core

    def remote(src, dst, send, recv, device):
        return pltpu.make_async_remote_copy(
            src_ref=src, dst_ref=dst, send_sem=send, recv_sem=recv,
            device_id=device, device_id_type=MESH,
        )

    barrier = pltpu.get_barrier_semaphore()
    peers = [(owner(k), salt) for k in range(1, OWNERS)]
    peers += [(ublk, line(1, pc)), (ublk, line(3, pc)), (ublk, line(0, 1 - pc))]
    for device in peers:
        pl.semaphore_signal(barrier, inc=1, device_id=device, device_id_type=MESH)

    def select(source, who, start, size, first=False, last=None):
        part = source[pl.ds(start, size)]
        part_t = part.T
        outer = jnp.dot(part_t, part, preferred_element_type=F32)
        if first:
            gram[...] = outer
        else:
            gram[...] += outer
        if last is not None:
            last()
        base = who * SHARD + start
        for n in range(SLOTS // TILE):
            at = pl.ds(n * TILE, TILE)
            chosen = (users[:, at] - base) == lax.broadcasted_iota(jnp.int32, (size, TILE), 0)
            one_hot = jnp.where(chosen, 1.0, 0.0).astype(BF16)
            found = jnp.dot(part_t, one_hot, preferred_element_type=F32).astype(BF16)
            if not first:
                found = rows_t[:, at] + found
            if last is None:
                rows_t[:, at] = found
            else:
                rows[at] = found.T
                scaled_t[:, at] = (found.astype(F32) * weight[:, at]).astype(BF16)

    loads = [
        pltpu.make_async_copy(source, target, load_sem.at[n])
        for n, (source, target) in enumerate(
            ((shard_in, shard), (users_in, users), (items_in, items), (raw_in, raw))
        )
    ]
    for copy in loads:
        copy.start()
    for copy in loads:
        copy.wait()
    pl.semaphore_wait(barrier, len(peers))

    partner = (ublk, line(0, 1 - pc))

    def moved(place, h):
        start = h * CHUNK if isinstance(h, int) else pl.multiple_of(h * CHUNK, CHUNK)
        piece = pl.ds(start, CHUNK)
        source, device = {
            UP: (shard, (ublk, line(1, pc))),
            DOWN: (shard, (ublk, line(3, pc))),
            PARTNER: (shard, partner),
            ACROSS: (block.at[UP + pc], (ublk, line(1 + 2 * pc, pc))),
            P_UP: (block.at[UP], partner),
            P_DOWN: (block.at[DOWN], partner),
            P_ACROSS: (block.at[ACROSS], partner),
        }[place]
        return remote(
            source.at[piece], block.at[place, piece], ag_send.at[place, h], ag_recv.at[place, h], device
        )

    whose = {
        PARTNER: line(0, 1 - pc), UP: line(3, pc), DOWN: line(1, pc), ACROSS: line(2, pc),
        P_UP: line(3, 1 - pc), P_DOWN: line(1, 1 - pc), P_ACROSS: line(2, 1 - pc),
    }

    def take(place, h, last=None):
        start = h * CHUNK if isinstance(h, int) else pl.multiple_of(h * CHUNK, CHUNK)
        select(block.at[place], whose[place], start, CHUNK, last=last)

    for h in range(CHUNKS):
        for place in (UP, DOWN, PARTNER):
            moved(place, h).start()

    gram_copies = [
        remote(
            gram.at[pl.ds(pl.multiple_of(owner(k) * GRAM_OWN, GRAM_OWN), GRAM_OWN)], gram_in.at[k],
            gram_send.at[k], gram_recv.at[k], (owner(k), salt),
        )
        for k in range(OWNERS) if k
    ]

    def send_gram():
        for copy in reversed(gram_copies):
            copy.start()

    select(shard, salt, 0, UNIT, first=True)
    select(shard, salt, UNIT, UNIT)

    for g in range(GROUPS):
        for k in range(OWNERS):
            place = items[...] - (owner(k) * OWN + g * HALF)
            chosen = place == lax.broadcasted_iota(jnp.int32, (HALF, SLOTS), 0)
            mask[pl.ds(g * GROUP + k * HALF, HALF)] = jnp.where(chosen, 1.0, 0.0).astype(BF16)
    alive = lax.broadcasted_iota(jnp.int32, (1, SLOTS), 1) < live[0, 0]
    weight[...] = jnp.where(alive, raw[...], 0.0)
    confid[...] = jnp.where(alive, 1.0 + raw[...], 0.0)

    for unit in range(SHARD // UNIT):
        for h in range(unit * UNIT // CHUNK, (unit + 1) * UNIT // CHUNK):
            moved(PARTNER, h).wait_recv()
        select(block.at[PARTNER], whose[PARTNER], unit * UNIT, UNIT)

    def near(h, carry):
        for place in (UP, DOWN):
            moved(place, h).wait_recv()
        for place in (P_UP, P_DOWN, ACROSS):
            moved(place, h).start()
        take(UP, h)
        take(DOWN, h)
        for place in (P_UP, P_DOWN):
            moved(place, h).wait_recv()
            take(place, h)
        return carry

    lax.fori_loop(0, CHUNKS, near, 0)

    def hand_over(h):
        moved(ACROSS, h).wait_recv()
        moved(P_ACROSS, h).start()

    def far(h, carry):
        take(ACROSS, h)
        hand_over(h + 1)
        moved(P_ACROSS, h).wait_recv()
        take(P_ACROSS, h)
        return carry

    hand_over(0)
    lax.fori_loop(0, CHUNKS - 1, far, 0)
    take(ACROSS, CHUNKS - 1)
    moved(P_ACROSS, CHUNKS - 1).wait_recv()
    take(P_ACROSS, CHUNKS - 1, last=send_gram)

    upper = confid[...].astype(BF16)
    lower = (confid[...] - upper.astype(F32)).astype(BF16)
    rhs_copies = {}
    for g in range(GROUPS):
        at = pl.ds(g * GROUP, GROUP)
        parts = []
        for level in (upper, lower):
            for n in range(SLOTS // TILE):
                cols = pl.ds(n * TILE, TILE)
                terms[at, cols] = jnp.where(
                    mask[at, cols] != 0, level[:, n * TILE:(n + 1) * TILE], jnp.zeros((), BF16)
                )
            parts.append(jnp.dot(terms[at], rows[...], preferred_element_type=F32))
        rhs[at] = parts[0] + parts[1]
        for k in FAR_FIRST:
            rhs_copies[g, k] = remote(
                rhs.at[pl.ds(g * GROUP + k * HALF, HALF)], rhs_in.at[g, k],
                rhs_send.at[g, k], rhs_recv.at[g, k], (owner(k), salt),
            )
            rhs_copies[g, k].start()

    own_rows = pl.ds(pl.multiple_of(ublk * GRAM_OWN, GRAM_OWN), GRAM_OWN)
    total = gram[own_rows]
    for k in range(1, OWNERS):
        gram_copies[k - 1].wait_recv()
        total = total + gram_in[k]
    gram_own[...] = total
    gram_sum[own_rows] = total
    gall_copies = [
        remote(
            gram_own, gram_sum.at[own_rows], gall_send.at[k], gall_recv.at[k], (owner(k), salt)
        )
        for k in range(OWNERS) if k
    ]

    dir_copies = {}
    loc_copies = {}
    for g in range(GROUPS):
        for k in range(1, OWNERS):
            dir_copies[g, k] = remote(
                whole_dir.at[pl.ds(g * GROUP, HALF)], whole_dir.at[pl.ds(g * GROUP + k * HALF, HALF)],
                dir_send.at[g], dir_recv.at[g, k // (OWNERS // 2)], (owner(k, -1), salt),
            )
            loc_copies[g, k] = remote(
                out_terms.at[pl.ds(g * GROUP + k * HALF, HALF)], in_terms.at[g, k],
                loc_send.at[g], loc_recv.at[g], (owner(k), salt),
            )

    dir_waits = {}
    dir_all = {}
    loc_all = {}
    for g in range(GROUPS):
        for part, places in enumerate(PARTS):
            first = max(places[0], 1)
            rest = whole_dir.at[pl.ds(g * GROUP + first * HALF, (places[-1] + 1 - first) * HALF)]
            dir_waits[g, places[0]] = remote(rest, rest, dir_send.at[g], dir_recv.at[g, part], partner)
        rest = whole_dir.at[pl.ds(g * GROUP + HALF, GROUP - HALF)]
        dir_all[g] = remote(rest, rest, dir_send.at[g], dir_recv.at[g, 0], partner)
        others = in_terms.at[g, pl.ds(1, OWNERS - 1)]
        loc_all[g] = remote(others, others, loc_send.at[g], loc_recv.at[g], partner)

    def send_direction(g, p):
        direction[pl.ds(g * HALF, HALF)] = p
        whole_dir[pl.ds(g * GROUP, HALF)] = p.astype(BF16)
        for k in FAR_FIRST:
            dir_copies[g, k].start()

    for g in range(GROUPS):
        own = pl.ds(g * HALF, HALF)
        total = rhs[pl.ds(g * GROUP, HALF)]
        for k in range(1, OWNERS):
            rhs_copies[g, k].wait_recv()
            total = total + rhs_in[g, k]
        send_direction(g, total)
        r_out[own] = total
        x_out[own] = jnp.zeros_like(total)
        if g == 0:
            for copy in reversed(gall_copies):
                copy.start()

    def iteration(t, carry):
        for g in range(GROUPS):
            for sub in PARTS:
                at = pl.ds(g * GROUP + sub[0] * HALF, len(sub) * HALF)
                dir_waits[g, sub[0]].wait_recv()
                for n in range(SLOTS // TILE):
                    cols = pl.ds(n * TILE, TILE)
                    along = jnp.dot(whole_dir[at], scaled_t[:, cols], preferred_element_type=F32)
                    terms[at, cols] = jnp.where(mask[at, cols] != 0, along.astype(BF16), jnp.zeros((), BF16))
                local = jnp.dot(terms[at], rows[...], preferred_element_type=F32)
                if sub[0] == 0:
                    own_terms[pl.ds(g * HALF, HALF)] = local[:HALF]
                out_terms[at] = local.astype(BF16)
                for k in reversed(sub):
                    if k:
                        loc_copies[g, k].start()

        @pl.when(t == 0)
        def _():
            for copy in gall_copies:
                copy.wait_recv()

        for g in range(GROUPS):
            own = pl.ds(g * HALF, HALF)
            p = direction[own]
            r = r_out[own]
            norm_now = jnp.sum(r * r, axis=1, keepdims=True)
            image = jnp.dot(p, gram_sum[...], precision=lax.Precision.HIGHEST, preferred_element_type=F32)
            image = image + REG * p + own_terms[own]
            dir_all[g].wait_send()
            loc_all[g].wait_recv()
            for k in range(1, OWNERS):
                image = image + in_terms[g, k].astype(F32)
            alpha = norm_now / (jnp.sum(p * image, axis=1, keepdims=True) + EPS)
            x_out[own] += alpha * p
            r = r - alpha * image
            r_out[own] = r
            norm_next = jnp.sum(r * r, axis=1, keepdims=True)

            @pl.when(t < ITERS - 1)
            def _():
                send_direction(g, r + (norm_next / (norm_now + EPS)) * p)

            loc_all[g].wait_send()
        return carry

    lax.fori_loop(0, ITERS, iteration, 0)

    for place in range(SALT - 1):
        for h in range(CHUNKS):
            moved(place, h).wait_send()
    for copy in gram_copies + gall_copies + list(rhs_copies.values()):
        copy.wait_send()


def body(user_factors, tile_users, tile_items, tile_weight, live_count):
    vmem = pl.BlockSpec(memory_space=pltpu.VMEM)
    dma = pltpu.SemaphoreType.DMA
    found, left = pl.pallas_call(
        kernel,
        name="als_cg",
        out_shape=(jax.ShapeDtypeStruct((OWN, RANK), F32), jax.ShapeDtypeStruct((OWN, RANK), F32)),
        in_specs=[pl.BlockSpec(memory_space=pl.ANY)] * 4 + [pl.BlockSpec(memory_space=pltpu.SMEM)],
        out_specs=(vmem, vmem),
        scratch_shapes=[
            pltpu.VMEM((SHARD, RANK), BF16),
            pltpu.VMEM((1, SLOTS), jnp.int32),
            pltpu.VMEM((1, SLOTS), jnp.int32),
            pltpu.VMEM((1, SLOTS), F32),
            dma((4,)),
            pltpu.VMEM((SALT - 1, SHARD, RANK), BF16),
            pltpu.VMEM((1, SLOTS), F32),
            pltpu.VMEM((1, SLOTS), F32),
            pltpu.VMEM((RANK, SLOTS), BF16),
            pltpu.VMEM((RANK, SLOTS), BF16),
            pltpu.VMEM((SLOTS, RANK), BF16),
            pltpu.VMEM((ITEMS, SLOTS), BF16),
            pltpu.VMEM((ITEMS, SLOTS), BF16),
            pltpu.VMEM((RANK, RANK), F32),
            pltpu.VMEM((RANK, RANK), F32),
            pltpu.VMEM((OWNERS, GRAM_OWN, RANK), F32),
            pltpu.VMEM((GRAM_OWN, RANK), F32),
            pltpu.VMEM((ITEMS, RANK), F32),
            pltpu.VMEM((GROUPS, OWNERS, HALF, RANK), F32),
            pltpu.VMEM((ITEMS, RANK), BF16),
            pltpu.VMEM((OWN, RANK), F32),
            pltpu.VMEM((OWN, RANK), F32),
            pltpu.VMEM((ITEMS, RANK), BF16),
            pltpu.VMEM((GROUPS, OWNERS, HALF, RANK), BF16),
            dma((SALT - 1, CHUNKS)), dma((SALT - 1, CHUNKS)),
            dma((OWNERS,)), dma((OWNERS,)), dma((OWNERS,)), dma((OWNERS,)),
            dma((GROUPS, OWNERS)), dma((GROUPS, OWNERS)),
            dma((GROUPS,)), dma((GROUPS, len(PARTS))), dma((GROUPS,)), dma((GROUPS,)),
        ],
        compiler_params=pltpu.CompilerParams(
            collective_id=0, has_side_effects=True, vmem_limit_bytes=56 * 2**20
        ),
    )(user_factors[0], tile_users[0], tile_items[0], tile_weight[0], live_count)
    return (found[None], left[None])


def solution(mesh):
    return jax.shard_map(
        body,
        mesh=mesh,
        in_specs=(
            P("ublk", "salt", None),
            P("ublk", "salt", None),
            P("ublk", "salt", None),
            P("ublk", "salt", None),
            P("ublk", "salt"),
        ),
        out_specs=(P("salt", "ublk", None), P("salt", "ublk", None)),
        check_vma=False,
    )
```

```python
import jax
import jax.numpy as jnp
from jax import lax
from jax.experimental import pallas as pl
from jax.experimental.pallas import tpu as pltpu
from jax.sharding import PartitionSpec as P

ITERS = 8
REG = 1.0
EPS = 1e-06

X = 4
OWNERS = X * X
OWN = 32
RANK = 256
ITEMS = OWNERS * OWN
SLOTS = 4096
SHARD = 1024
SALT = 8
CHUNKS = 4
CHUNK = SHARD // CHUNKS
TILE = 1024
GRAM_OWN = RANK // OWNERS

F32 = jnp.float32
BF16 = jnp.bfloat16
MESH = pl.DeviceIdType.MESH


def ring(a):
    return min(a, X - a)


OFFSETS = sorted(
    [(dx, dz) for dx in range(X) for dz in range(X)],
    key=lambda o: (ring(o[0]) + ring(o[1]), o),
)
FAR_FIRST = list(range(OWNERS - 1, 0, -1))
GROUPS = 2
HALF = OWN // GROUPS
GROUP = OWNERS * HALF
PARTS = (range(0, OWNERS // 2), range(OWNERS // 2, OWNERS))
UNIT = 512

PARTNER, UP, DOWN, ACROSS, P_UP, P_DOWN, P_ACROSS = range(7)


def kernel(
    shard_in, users_in, items_in, raw_in, live,
    both_out,
    shard, users, items, raw, load_sem, block, weight, confid, rows_t, scaled_t, rows, mask, terms, gram, gram_sum, gram_in, gram_own,
    rhs, rhs_in, whole_dir, direction, own_terms, out_terms, in_terms,
    ag_send, ag_recv, gram_send, gram_recv, gall_send, gall_recv,
    rhs_send, rhs_recv, dir_send, dir_recv, loc_send, loc_recv,
):
    x_out, r_out = both_out.at[0], both_out.at[1]
    ublk = lax.axis_index("ublk")
    salt = lax.axis_index("salt")
    px, pz = lax.div(ublk, X), lax.rem(ublk, X)
    py, pc = lax.div(salt, 2), lax.rem(salt, 2)

    def owner(k, sign=1):
        dx, dz = OFFSETS[k]
        return lax.rem(px + sign * dx + X, X) * X + lax.rem(pz + sign * dz + X, X)

    def line(dy, core):
        return lax.rem(py + dy, X) * 2 + core

    def remote(src, dst, send, recv, device):
        return pltpu.make_async_remote_copy(
            src_ref=src, dst_ref=dst, send_sem=send, recv_sem=recv,
            device_id=device, device_id_type=MESH,
        )

    barrier = pltpu.get_barrier_semaphore()
    peers = [(owner(k), salt) for k in range(1, OWNERS)]
    peers += [(ublk, line(1, pc)), (ublk, line(3, pc)), (ublk, line(0, 1 - pc))]
    for device in peers:
        pl.semaphore_signal(barrier, inc=1, device_id=device, device_id_type=MESH)

    def select(source, who, start, size, first=False, last=None):
        part = source[pl.ds(start, size)]
        part_t = part.T
        outer = jnp.dot(part_t, part, preferred_element_type=F32)
        if first:
            gram[...] = outer
        else:
            gram[...] += outer
        if last is not None:
            last()
        base = who * SHARD + start
        for n in range(SLOTS // TILE):
            at = pl.ds(n * TILE, TILE)
            chosen = (users[:, at] - base) == lax.broadcasted_iota(jnp.int32, (size, TILE), 0)
            one_hot = jnp.where(chosen, 1.0, 0.0).astype(BF16)
            found = jnp.dot(part_t, one_hot, preferred_element_type=F32).astype(BF16)
            if not first:
                found = rows_t[:, at] + found
            if last is None:
                rows_t[:, at] = found
            else:
                rows[at] = found.T
                scaled_t[:, at] = (found.astype(F32) * weight[:, at]).astype(BF16)

    loads = [
        pltpu.make_async_copy(source, target, load_sem.at[n])
        for n, (source, target) in enumerate(
            ((shard_in, shard), (users_in, users), (items_in, items), (raw_in, raw))
        )
    ]
    for copy in loads:
        copy.start()
    for copy in loads:
        copy.wait()
    pl.semaphore_wait(barrier, len(peers))

    partner = (ublk, line(0, 1 - pc))

    def moved(place, h):
        start = h * CHUNK if isinstance(h, int) else pl.multiple_of(h * CHUNK, CHUNK)
        piece = pl.ds(start, CHUNK)
        source, device = {
            UP: (shard, (ublk, line(1, pc))),
            DOWN: (shard, (ublk, line(3, pc))),
            PARTNER: (shard, partner),
            ACROSS: (block.at[UP + pc], (ublk, line(1 + 2 * pc, pc))),
            P_UP: (block.at[UP], partner),
            P_DOWN: (block.at[DOWN], partner),
            P_ACROSS: (block.at[ACROSS], partner),
        }[place]
        return remote(
            source.at[piece], block.at[place, piece], ag_send.at[place, h], ag_recv.at[place, h], device
        )

    whose = {
        PARTNER: line(0, 1 - pc), UP: line(3, pc), DOWN: line(1, pc), ACROSS: line(2, pc),
        P_UP: line(3, 1 - pc), P_DOWN: line(1, 1 - pc), P_ACROSS: line(2, 1 - pc),
    }

    def take(place, h, last=None):
        start = h * CHUNK if isinstance(h, int) else pl.multiple_of(h * CHUNK, CHUNK)
        select(block.at[place], whose[place], start, CHUNK, last=last)

    for h in range(CHUNKS):
        for place in (UP, DOWN, PARTNER):
            moved(place, h).start()

    gram_copies = [
        remote(
            gram.at[pl.ds(pl.multiple_of(owner(k) * GRAM_OWN, GRAM_OWN), GRAM_OWN)], gram_in.at[k],
            gram_send.at[k], gram_recv.at[k], (owner(k), salt),
        )
        for k in range(OWNERS) if k
    ]

    def send_gram():
        for copy in reversed(gram_copies):
            copy.start()

    select(shard, salt, 0, UNIT, first=True)
    select(shard, salt, UNIT, UNIT)

    for g in range(GROUPS):
        for k in range(OWNERS):
            place = items[...] - (owner(k) * OWN + g * HALF)
            chosen = place == lax.broadcasted_iota(jnp.int32, (HALF, SLOTS), 0)
            mask[pl.ds(g * GROUP + k * HALF, HALF)] = jnp.where(chosen, 1.0, 0.0).astype(BF16)
    alive = lax.broadcasted_iota(jnp.int32, (1, SLOTS), 1) < live[0, 0]
    weight[...] = jnp.where(alive, raw[...], 0.0)
    confid[...] = jnp.where(alive, 1.0 + raw[...], 0.0)

    for unit in range(SHARD // UNIT):
        for h in range(unit * UNIT // CHUNK, (unit + 1) * UNIT // CHUNK):
            moved(PARTNER, h).wait_recv()
        select(block.at[PARTNER], whose[PARTNER], unit * UNIT, UNIT)

    def near(h, carry):
        for place in (UP, DOWN):
            moved(place, h).wait_recv()
        for place in (P_UP, P_DOWN, ACROSS):
            moved(place, h).start()
        take(UP, h)
        take(DOWN, h)
        for place in (P_UP, P_DOWN):
            moved(place, h).wait_recv()
            take(place, h)
        return carry

    lax.fori_loop(0, CHUNKS, near, 0)

    def hand_over(h):
        moved(ACROSS, h).wait_recv()
        moved(P_ACROSS, h).start()

    def far(h, carry):
        take(ACROSS, h)
        hand_over(h + 1)
        moved(P_ACROSS, h).wait_recv()
        take(P_ACROSS, h)
        return carry

    hand_over(0)
    lax.fori_loop(0, CHUNKS - 1, far, 0)
    take(ACROSS, CHUNKS - 1)
    moved(P_ACROSS, CHUNKS - 1).wait_recv()
    take(P_ACROSS, CHUNKS - 1, last=send_gram)

    upper = confid[...].astype(BF16)
    lower = (confid[...] - upper.astype(F32)).astype(BF16)
    rhs_copies = {}
    for g in range(GROUPS):
        at = pl.ds(g * GROUP, GROUP)
        parts = []
        for level in (upper, lower):
            for n in range(SLOTS // TILE):
                cols = pl.ds(n * TILE, TILE)
                terms[at, cols] = jnp.where(
                    mask[at, cols] != 0, level[:, n * TILE:(n + 1) * TILE], jnp.zeros((), BF16)
                )
            parts.append(jnp.dot(terms[at], rows[...], preferred_element_type=F32))
        rhs[at] = parts[0] + parts[1]
        for k in FAR_FIRST:
            rhs_copies[g, k] = remote(
                rhs.at[pl.ds(g * GROUP + k * HALF, HALF)], rhs_in.at[g, k],
                rhs_send.at[g, k], rhs_recv.at[g, k], (owner(k), salt),
            )
            rhs_copies[g, k].start()

    own_rows = pl.ds(pl.multiple_of(ublk * GRAM_OWN, GRAM_OWN), GRAM_OWN)
    total = gram[own_rows]
    for k in range(1, OWNERS):
        gram_copies[k - 1].wait_recv()
        total = total + gram_in[k]
    gram_own[...] = total
    gram_sum[own_rows] = total
    gall_copies = [
        remote(
            gram_own, gram_sum.at[own_rows], gall_send.at[k], gall_recv.at[k], (owner(k), salt)
        )
        for k in range(OWNERS) if k
    ]

    dir_copies = {}
    loc_copies = {}
    for g in range(GROUPS):
        for k in range(1, OWNERS):
            dir_copies[g, k] = remote(
                whole_dir.at[pl.ds(g * GROUP, HALF)], whole_dir.at[pl.ds(g * GROUP + k * HALF, HALF)],
                dir_send.at[g], dir_recv.at[g, k // (OWNERS // 2)], (owner(k, -1), salt),
            )
            loc_copies[g, k] = remote(
                out_terms.at[pl.ds(g * GROUP + k * HALF, HALF)], in_terms.at[g, k],
                loc_send.at[g], loc_recv.at[g], (owner(k), salt),
            )

    dir_waits = {}
    dir_all = {}
    loc_all = {}
    for g in range(GROUPS):
        for part, places in enumerate(PARTS):
            first = max(places[0], 1)
            rest = whole_dir.at[pl.ds(g * GROUP + first * HALF, (places[-1] + 1 - first) * HALF)]
            dir_waits[g, places[0]] = remote(rest, rest, dir_send.at[g], dir_recv.at[g, part], partner)
        rest = whole_dir.at[pl.ds(g * GROUP + HALF, GROUP - HALF)]
        dir_all[g] = remote(rest, rest, dir_send.at[g], dir_recv.at[g, 0], partner)
        others = in_terms.at[g, pl.ds(1, OWNERS - 1)]
        loc_all[g] = remote(others, others, loc_send.at[g], loc_recv.at[g], partner)

    def send_direction(g, p):
        direction[pl.ds(g * HALF, HALF)] = p
        whole_dir[pl.ds(g * GROUP, HALF)] = p.astype(BF16)
        for k in FAR_FIRST:
            dir_copies[g, k].start()

    for g in range(GROUPS):
        own = pl.ds(g * HALF, HALF)
        total = rhs[pl.ds(g * GROUP, HALF)]
        for k in range(1, OWNERS):
            rhs_copies[g, k].wait_recv()
            total = total + rhs_in[g, k]
        send_direction(g, total)
        r_out[own] = total
        x_out[own] = jnp.zeros_like(total)

    for copy in reversed(gall_copies):
        copy.start()

    def iteration(t, carry):
        for g in range(GROUPS):
            for sub in PARTS:
                at = pl.ds(g * GROUP + sub[0] * HALF, len(sub) * HALF)
                dir_waits[g, sub[0]].wait_recv()
                for n in range(SLOTS // TILE):
                    cols = pl.ds(n * TILE, TILE)
                    along = jnp.dot(whole_dir[at], scaled_t[:, cols], preferred_element_type=F32)
                    terms[at, cols] = jnp.where(mask[at, cols] != 0, along.astype(BF16), jnp.zeros((), BF16))
                local = jnp.dot(terms[at], rows[...], preferred_element_type=F32)
                if sub[0] == 0:
                    own_terms[pl.ds(g * HALF, HALF)] = local[:HALF]
                out_terms[at] = local.astype(BF16)
                for k in reversed(sub):
                    if k:
                        loc_copies[g, k].start()

        @pl.when(t == 0)
        def _():
            for copy in gall_copies:
                copy.wait_recv()

        for g in range(GROUPS):
            own = pl.ds(g * HALF, HALF)
            p = direction[own]
            r = r_out[own]
            norm_now = jnp.sum(r * r, axis=1, keepdims=True)
            image = jnp.dot(p, gram_sum[...], precision=lax.Precision.HIGHEST, preferred_element_type=F32)
            image = image + REG * p + own_terms[own]
            dir_all[g].wait_send()
            loc_all[g].wait_recv()
            for k in range(1, OWNERS):
                image = image + in_terms[g, k].astype(F32)
            alpha = norm_now / (jnp.sum(p * image, axis=1, keepdims=True) + EPS)
            x_out[own] += alpha * p
            r = r - alpha * image
            r_out[own] = r
            norm_next = jnp.sum(r * r, axis=1, keepdims=True)

            @pl.when(t < ITERS - 1)
            def _():
                send_direction(g, r + (norm_next / (norm_now + EPS)) * p)

            loc_all[g].wait_send()
        return carry

    lax.fori_loop(0, ITERS, iteration, 0)

    for place in range(SALT - 1):
        for h in range(CHUNKS):
            moved(place, h).wait_send()
    for copy in gram_copies + gall_copies + list(rhs_copies.values()):
        copy.wait_send()


def body(user_factors, tile_users, tile_items, tile_weight, live_count):
    vmem = pl.BlockSpec(memory_space=pltpu.VMEM)
    dma = pltpu.SemaphoreType.DMA
    both = pl.pallas_call(
        kernel,
        name="als_cg",
        out_shape=jax.ShapeDtypeStruct((2, OWN, RANK), F32),
        in_specs=[pl.BlockSpec(memory_space=pl.ANY)] * 4 + [pl.BlockSpec(memory_space=pltpu.SMEM)],
        out_specs=vmem,
        scratch_shapes=[
            pltpu.VMEM((SHARD, RANK), BF16),
            pltpu.VMEM((1, SLOTS), jnp.int32),
            pltpu.VMEM((1, SLOTS), jnp.int32),
            pltpu.VMEM((1, SLOTS), F32),
            dma((4,)),
            pltpu.VMEM((SALT - 1, SHARD, RANK), BF16),
            pltpu.VMEM((1, SLOTS), F32),
            pltpu.VMEM((1, SLOTS), F32),
            pltpu.VMEM((RANK, SLOTS), BF16),
            pltpu.VMEM((RANK, SLOTS), BF16),
            pltpu.VMEM((SLOTS, RANK), BF16),
            pltpu.VMEM((ITEMS, SLOTS), BF16),
            pltpu.VMEM((ITEMS, SLOTS), BF16),
            pltpu.VMEM((RANK, RANK), F32),
            pltpu.VMEM((RANK, RANK), F32),
            pltpu.VMEM((OWNERS, GRAM_OWN, RANK), F32),
            pltpu.VMEM((GRAM_OWN, RANK), F32),
            pltpu.VMEM((ITEMS, RANK), F32),
            pltpu.VMEM((GROUPS, OWNERS, HALF, RANK), F32),
            pltpu.VMEM((ITEMS, RANK), BF16),
            pltpu.VMEM((OWN, RANK), F32),
            pltpu.VMEM((OWN, RANK), F32),
            pltpu.VMEM((ITEMS, RANK), BF16),
            pltpu.VMEM((GROUPS, OWNERS, HALF, RANK), BF16),
            dma((SALT - 1, CHUNKS)), dma((SALT - 1, CHUNKS)),
            dma((OWNERS,)), dma((OWNERS,)), dma((OWNERS,)), dma((OWNERS,)),
            dma((GROUPS, OWNERS)), dma((GROUPS, OWNERS)),
            dma((GROUPS,)), dma((GROUPS, len(PARTS))), dma((GROUPS,)), dma((GROUPS,)),
        ],
        compiler_params=pltpu.CompilerParams(
            collective_id=0, has_side_effects=True, vmem_limit_bytes=56 * 2**20
        ),
    )(user_factors[0], tile_users[0], tile_items[0], tile_weight[0], live_count)
    return (both[:1], both[1:])


def solution(mesh):
    return jax.shard_map(
        body,
        mesh=mesh,
        in_specs=(
            P("ublk", "salt", None),
            P("ublk", "salt", None),
            P("ublk", "salt", None),
            P("ublk", "salt", None),
            P("ublk", "salt"),
        ),
        out_specs=(P("salt", "ublk", None), P("salt", "ublk", None)),
        check_vma=False,
    )
```

```python
import jax
import jax.numpy as jnp
from jax import lax
from jax.experimental import pallas as pl
from jax.experimental.pallas import tpu as pltpu
from jax.sharding import PartitionSpec as P

ITERS = 8
REG = 1.0
EPS = 1e-06

X = 4
OWNERS = X * X
OWN = 32
RANK = 256
ITEMS = OWNERS * OWN
SLOTS = 4096
SHARD = 1024
SALT = 8
CHUNKS = 4
CHUNK = SHARD // CHUNKS
TILE = 1024
GRAM_OWN = RANK // OWNERS

F32 = jnp.float32
BF16 = jnp.bfloat16
MESH = pl.DeviceIdType.MESH


def ring(a):
    return min(a, X - a)


OFFSETS = sorted(
    [(dx, dz) for dx in range(X) for dz in range(X)],
    key=lambda o: (ring(o[0]) + ring(o[1]), o),
)
FAR_FIRST = list(range(OWNERS - 1, 0, -1))
GROUPS = 2
HALF = OWN // GROUPS
GROUP = OWNERS * HALF
PARTS = (range(0, OWNERS // 2), range(OWNERS // 2, OWNERS))
UNIT = 512

PARTNER, UP, DOWN, ACROSS, P_UP, P_DOWN, P_ACROSS = range(7)


def kernel(
    shard_in, users_in, items_in, raw_in, live,
    both_out,
    shard, users, items, raw, load_sem, block, weight, confid, rows_t, scaled_t, rows, mask, terms, gram, gram_sum, gram_in, gram_own,
    rhs, rhs_in, whole_dir, direction, own_terms, out_terms, in_terms,
    ag_send, ag_recv, gram_send, gram_recv, gall_send, gall_recv,
    rhs_send, rhs_recv, dir_send, dir_recv, loc_send, loc_recv,
):
    x_out, r_out = both_out.at[0], both_out.at[1]
    ublk = lax.axis_index("ublk")
    salt = lax.axis_index("salt")
    px, pz = lax.div(ublk, X), lax.rem(ublk, X)
    py, pc = lax.div(salt, 2), lax.rem(salt, 2)

    def owner(k, sign=1):
        dx, dz = OFFSETS[k]
        return lax.rem(px + sign * dx + X, X) * X + lax.rem(pz + sign * dz + X, X)

    def line(dy, core):
        return lax.rem(py + dy, X) * 2 + core

    def remote(src, dst, send, recv, device):
        return pltpu.make_async_remote_copy(
            src_ref=src, dst_ref=dst, send_sem=send, recv_sem=recv,
            device_id=device, device_id_type=MESH,
        )

    barrier = pltpu.get_barrier_semaphore()
    peers = [(owner(k), salt) for k in range(1, OWNERS)]
    peers += [(ublk, line(1, pc)), (ublk, line(3, pc)), (ublk, line(0, 1 - pc))]
    for device in peers:
        pl.semaphore_signal(barrier, inc=1, device_id=device, device_id_type=MESH)

    def select(source, who, start, size, first=False, last=None):
        part = source[pl.ds(start, size)]
        part_t = part.T
        outer = jnp.dot(part_t, part, preferred_element_type=F32)
        if first:
            gram[...] = outer
        else:
            gram[...] += outer
        if last is not None:
            last()
        base = who * SHARD + start
        for n in range(SLOTS // TILE):
            at = pl.ds(n * TILE, TILE)
            chosen = (users[:, at] - base) == lax.broadcasted_iota(jnp.int32, (size, TILE), 0)
            one_hot = jnp.where(chosen, 1.0, 0.0).astype(BF16)
            found = jnp.dot(part_t, one_hot, preferred_element_type=F32).astype(BF16)
            if not first:
                found = rows_t[:, at] + found
            if last is None:
                rows_t[:, at] = found
            else:
                rows[at] = found.T
                scaled_t[:, at] = (found.astype(F32) * weight[:, at]).astype(BF16)

    loads = [
        pltpu.make_async_copy(source, target, load_sem.at[n])
        for n, (source, target) in enumerate(
            ((shard_in, shard), (users_in, users), (items_in, items), (raw_in, raw))
        )
    ]
    for copy in loads:
        copy.start()
    for copy in loads:
        copy.wait()
    pl.semaphore_wait(barrier, len(peers))

    partner = (ublk, line(0, 1 - pc))

    def moved(place, h):
        start = h * CHUNK if isinstance(h, int) else pl.multiple_of(h * CHUNK, CHUNK)
        piece = pl.ds(start, CHUNK)
        source, device = {
            UP: (shard, (ublk, line(1, pc))),
            DOWN: (shard, (ublk, line(3, pc))),
            PARTNER: (shard, partner),
            ACROSS: (block.at[UP + pc], (ublk, line(1 + 2 * pc, pc))),
            P_UP: (block.at[UP], partner),
            P_DOWN: (block.at[DOWN], partner),
            P_ACROSS: (block.at[ACROSS], partner),
        }[place]
        return remote(
            source.at[piece], block.at[place, piece], ag_send.at[place, h], ag_recv.at[place, h], device
        )

    whose = {
        PARTNER: line(0, 1 - pc), UP: line(3, pc), DOWN: line(1, pc), ACROSS: line(2, pc),
        P_UP: line(3, 1 - pc), P_DOWN: line(1, 1 - pc), P_ACROSS: line(2, 1 - pc),
    }

    def take(place, h, last=None):
        start = h * CHUNK if isinstance(h, int) else pl.multiple_of(h * CHUNK, CHUNK)
        select(block.at[place], whose[place], start, CHUNK, last=last)

    for h in range(CHUNKS):
        for place in (UP, DOWN, PARTNER):
            moved(place, h).start()

    gram_copies = [
        remote(
            gram.at[pl.ds(pl.multiple_of(owner(k) * GRAM_OWN, GRAM_OWN), GRAM_OWN)], gram_in.at[k],
            gram_send.at[k], gram_recv.at[k], (owner(k), salt),
        )
        for k in range(OWNERS) if k
    ]

    def send_gram():
        for copy in reversed(gram_copies):
            copy.start()

    select(shard, salt, 0, UNIT, first=True)
    select(shard, salt, UNIT, UNIT)

    for g in range(GROUPS):
        for k in range(OWNERS):
            place = items[...] - (owner(k) * OWN + g * HALF)
            chosen = place == lax.broadcasted_iota(jnp.int32, (HALF, SLOTS), 0)
            mask[pl.ds(g * GROUP + k * HALF, HALF)] = jnp.where(chosen, 1.0, 0.0).astype(BF16)
    alive = lax.broadcasted_iota(jnp.int32, (1, SLOTS), 1) < live[0, 0]
    weight[...] = jnp.where(alive, raw[...], 0.0)
    confid[...] = jnp.where(alive, 1.0 + raw[...], 0.0)

    for unit in range(SHARD // UNIT):
        for h in range(unit * UNIT // CHUNK, (unit + 1) * UNIT // CHUNK):
            moved(PARTNER, h).wait_recv()
        select(block.at[PARTNER], whose[PARTNER], unit * UNIT, UNIT)

    def near(h, carry):
        for place in (UP, DOWN):
            moved(place, h).wait_recv()
        for place in (ACROSS, P_UP, P_DOWN):
            moved(place, h).start()
        take(UP, h)
        take(DOWN, h)
        for place in (P_UP, P_DOWN):
            moved(place, h).wait_recv()
            take(place, h)
        return carry

    lax.fori_loop(0, CHUNKS, near, 0)

    def hand_over(h):
        moved(ACROSS, h).wait_recv()
        moved(P_ACROSS, h).start()

    def far(h, carry):
        take(ACROSS, h)
        hand_over(h + 1)
        moved(P_ACROSS, h).wait_recv()
        take(P_ACROSS, h)
        return carry

    hand_over(0)
    lax.fori_loop(0, CHUNKS - 1, far, 0)
    take(ACROSS, CHUNKS - 1)
    moved(P_ACROSS, CHUNKS - 1).wait_recv()
    take(P_ACROSS, CHUNKS - 1, last=send_gram)

    upper = confid[...].astype(BF16)
    lower = (confid[...] - upper.astype(F32)).astype(BF16)
    rhs_copies = {}
    for g in range(GROUPS):
        at = pl.ds(g * GROUP, GROUP)
        parts = []
        for level in (upper, lower):
            for n in range(SLOTS // TILE):
                cols = pl.ds(n * TILE, TILE)
                terms[at, cols] = jnp.where(
                    mask[at, cols] != 0, level[:, n * TILE:(n + 1) * TILE], jnp.zeros((), BF16)
                )
            parts.append(jnp.dot(terms[at], rows[...], preferred_element_type=F32))
        rhs[at] = parts[0] + parts[1]
        for k in FAR_FIRST:
            rhs_copies[g, k] = remote(
                rhs.at[pl.ds(g * GROUP + k * HALF, HALF)], rhs_in.at[g, k],
                rhs_send.at[g, k], rhs_recv.at[g, k], (owner(k), salt),
            )
            rhs_copies[g, k].start()

    own_rows = pl.ds(pl.multiple_of(ublk * GRAM_OWN, GRAM_OWN), GRAM_OWN)
    total = gram[own_rows]
    for k in range(1, OWNERS):
        gram_copies[k - 1].wait_recv()
        total = total + gram_in[k]
    gram_own[...] = total
    gram_sum[own_rows] = total
    gall_copies = [
        remote(
            gram_own, gram_sum.at[own_rows], gall_send.at[k], gall_recv.at[k], (owner(k), salt)
        )
        for k in range(OWNERS) if k
    ]

    dir_copies = {}
    loc_copies = {}
    for g in range(GROUPS):
        for k in range(1, OWNERS):
            dir_copies[g, k] = remote(
                whole_dir.at[pl.ds(g * GROUP, HALF)], whole_dir.at[pl.ds(g * GROUP + k * HALF, HALF)],
                dir_send.at[g], dir_recv.at[g, k // (OWNERS // 2)], (owner(k, -1), salt),
            )
            loc_copies[g, k] = remote(
                out_terms.at[pl.ds(g * GROUP + k * HALF, HALF)], in_terms.at[g, k],
                loc_send.at[g], loc_recv.at[g], (owner(k), salt),
            )

    dir_waits = {}
    dir_all = {}
    loc_all = {}
    for g in range(GROUPS):
        for part, places in enumerate(PARTS):
            first = max(places[0], 1)
            rest = whole_dir.at[pl.ds(g * GROUP + first * HALF, (places[-1] + 1 - first) * HALF)]
            dir_waits[g, places[0]] = remote(rest, rest, dir_send.at[g], dir_recv.at[g, part], partner)
        rest = whole_dir.at[pl.ds(g * GROUP + HALF, GROUP - HALF)]
        dir_all[g] = remote(rest, rest, dir_send.at[g], dir_recv.at[g, 0], partner)
        others = in_terms.at[g, pl.ds(1, OWNERS - 1)]
        loc_all[g] = remote(others, others, loc_send.at[g], loc_recv.at[g], partner)

    def send_direction(g, p):
        direction[pl.ds(g * HALF, HALF)] = p
        whole_dir[pl.ds(g * GROUP, HALF)] = p.astype(BF16)
        for k in FAR_FIRST:
            dir_copies[g, k].start()

    for g in range(GROUPS):
        own = pl.ds(g * HALF, HALF)
        total = rhs[pl.ds(g * GROUP, HALF)]
        for k in range(1, OWNERS):
            rhs_copies[g, k].wait_recv()
            total = total + rhs_in[g, k]
        send_direction(g, total)
        r_out[own] = total
        x_out[own] = jnp.zeros_like(total)

    for copy in reversed(gall_copies):
        copy.start()

    def iteration(t, carry):
        for g in range(GROUPS):
            for sub in PARTS:
                at = pl.ds(g * GROUP + sub[0] * HALF, len(sub) * HALF)
                dir_waits[g, sub[0]].wait_recv()
                for n in range(SLOTS // TILE):
                    cols = pl.ds(n * TILE, TILE)
                    along = jnp.dot(whole_dir[at], scaled_t[:, cols], preferred_element_type=F32)
                    terms[at, cols] = jnp.where(mask[at, cols] != 0, along.astype(BF16), jnp.zeros((), BF16))
                local = jnp.dot(terms[at], rows[...], preferred_element_type=F32)
                if sub[0] == 0:
                    own_terms[pl.ds(g * HALF, HALF)] = local[:HALF]
                out_terms[at] = local.astype(BF16)
                for k in reversed(sub):
                    if k:
                        loc_copies[g, k].start()

        @pl.when(t == 0)
        def _():
            for copy in gall_copies:
                copy.wait_recv()

        for g in range(GROUPS):
            own = pl.ds(g * HALF, HALF)
            p = direction[own]
            r = r_out[own]
            norm_now = jnp.sum(r * r, axis=1, keepdims=True)
            image = jnp.dot(p, gram_sum[...], precision=lax.Precision.HIGHEST, preferred_element_type=F32)
            image = image + REG * p + own_terms[own]
            dir_all[g].wait_send()
            loc_all[g].wait_recv()
            for k in range(1, OWNERS):
                image = image + in_terms[g, k].astype(F32)
            alpha = norm_now / (jnp.sum(p * image, axis=1, keepdims=True) + EPS)
            x_out[own] += alpha * p
            r = r - alpha * image
            r_out[own] = r
            norm_next = jnp.sum(r * r, axis=1, keepdims=True)

            @pl.when(t < ITERS - 1)
            def _():
                send_direction(g, r + (norm_next / (norm_now + EPS)) * p)

            loc_all[g].wait_send()
        return carry

    lax.fori_loop(0, ITERS, iteration, 0)

    for place in range(SALT - 1):
        for h in range(CHUNKS):
            moved(place, h).wait_send()
    for copy in gram_copies + gall_copies + list(rhs_copies.values()):
        copy.wait_send()


def body(user_factors, tile_users, tile_items, tile_weight, live_count):
    vmem = pl.BlockSpec(memory_space=pltpu.VMEM)
    dma = pltpu.SemaphoreType.DMA
    both = pl.pallas_call(
        kernel,
        name="als_cg",
        out_shape=jax.ShapeDtypeStruct((2, OWN, RANK), F32),
        in_specs=[pl.BlockSpec(memory_space=pl.ANY)] * 4 + [pl.BlockSpec(memory_space=pltpu.SMEM)],
        out_specs=vmem,
        scratch_shapes=[
            pltpu.VMEM((SHARD, RANK), BF16),
            pltpu.VMEM((1, SLOTS), jnp.int32),
            pltpu.VMEM((1, SLOTS), jnp.int32),
            pltpu.VMEM((1, SLOTS), F32),
            dma((4,)),
            pltpu.VMEM((SALT - 1, SHARD, RANK), BF16),
            pltpu.VMEM((1, SLOTS), F32),
            pltpu.VMEM((1, SLOTS), F32),
            pltpu.VMEM((RANK, SLOTS), BF16),
            pltpu.VMEM((RANK, SLOTS), BF16),
            pltpu.VMEM((SLOTS, RANK), BF16),
            pltpu.VMEM((ITEMS, SLOTS), BF16),
            pltpu.VMEM((ITEMS, SLOTS), BF16),
            pltpu.VMEM((RANK, RANK), F32),
            pltpu.VMEM((RANK, RANK), F32),
            pltpu.VMEM((OWNERS, GRAM_OWN, RANK), F32),
            pltpu.VMEM((GRAM_OWN, RANK), F32),
            pltpu.VMEM((ITEMS, RANK), F32),
            pltpu.VMEM((GROUPS, OWNERS, HALF, RANK), F32),
            pltpu.VMEM((ITEMS, RANK), BF16),
            pltpu.VMEM((OWN, RANK), F32),
            pltpu.VMEM((OWN, RANK), F32),
            pltpu.VMEM((ITEMS, RANK), BF16),
            pltpu.VMEM((GROUPS, OWNERS, HALF, RANK), BF16),
            dma((SALT - 1, CHUNKS)), dma((SALT - 1, CHUNKS)),
            dma((OWNERS,)), dma((OWNERS,)), dma((OWNERS,)), dma((OWNERS,)),
            dma((GROUPS, OWNERS)), dma((GROUPS, OWNERS)),
            dma((GROUPS,)), dma((GROUPS, len(PARTS))), dma((GROUPS,)), dma((GROUPS,)),
        ],
        compiler_params=pltpu.CompilerParams(
            collective_id=0, has_side_effects=True, vmem_limit_bytes=56 * 2**20
        ),
    )(user_factors[0], tile_users[0], tile_items[0], tile_weight[0], live_count)
    return (both[:1], both[1:])


def solution(mesh):
    return jax.shard_map(
        body,
        mesh=mesh,
        in_specs=(
            P("ublk", "salt", None),
            P("ublk", "salt", None),
            P("ublk", "salt", None),
            P("ublk", "salt", None),
            P("ublk", "salt"),
        ),
        out_specs=(P("salt", "ublk", None), P("salt", "ublk", None)),
        check_vma=False,
    )
```
